128 devices in a mesh: src: 8 (over y, core), rcv: 16 (over x, z).
Axes of the slice: x: 4, y: 4, z: 4, core: 2. Of those that a mesh axis runs over, the one named last changes fastest.
Arguments:
- recorded: float32 [1024, 1024, 512], P('src', 'rcv'), may hold values from -16 to 16, as said below
- owner_map: int32 [64], replicated, may hold values from 0 to 127, as said below
Outputs:
- squares: bfloat16 [128, 2, 2, 1024, 1024], P(('src', 'rcv'))
The draws below stay inside these ranges and needn't reach their ends.
Inputs may be any that keep to these rules, and one draw needn't show every extreme that they name: `recorded`: every trace is noise times a trace amplitude of its own. `owner_map`: no device owns more than 2 frequencies, and some device owns exactly 2.
All inputs are finite; a program needn't handle non-finite values.
Results may differ from the reference program's by a relative error of at most 0.0076.
Values may be sent and summed in bfloat16 or wider, within the bound.
A program may use at most 192 MiB of HBM per device.

```python
import math
import jax
import jax.numpy as jnp
from jax import lax

S = 1024
R = 1024
NT = 512
FIRST = 4
CAP = 2
NDEV = 128
NF = 64


def draw_recorded(key, part):
    key_noise, key_gain = jax.random.split(jax.random.fold_in(key, 11))
    noise = jnp.clip(jax.random.normal(key_noise, (S, R, NT), jnp.float32), -5.0, 5.0)
    gains = jnp.exp(jax.random.uniform(key_gain, (S, R, 1), jnp.float32, math.log(0.3), math.log(3.0)))
    return noise * gains


def draw_owner_map(key, part):
    key_pairs, key_devices, key_bands = jax.random.split(jax.random.fold_in(key, 7), 3)
    lowest = max(1, -(-(NF - NDEV) // (CAP - 1)))
    highest = NF // CAP
    paired = jax.random.randint(key_pairs, (), lowest, highest + 1)
    position = jnp.arange(NF, dtype=jnp.int32)
    groups_of = jnp.where(position < CAP * paired, position // CAP, position - (CAP - 1) * paired)
    devices_order = jax.random.permutation(key_devices, NDEV).astype(jnp.int32)
    bands_order = jax.random.permutation(key_bands, NF)
    return jnp.zeros((NF,), jnp.int32).at[bands_order].set(devices_order[groups_of])


def setup_inputs(seed: int = 0) -> dict:
    splits = jax.random.split(jax.random.key(seed), 3)
    recorded = draw_recorded(jax.random.fold_in(splits[2], 71), 0)
    owner_map = draw_owner_map(jax.random.fold_in(splits[2], 71), 0)
    return dict(recorded=recorded, owner_map=owner_map)


WATER = 0.5

def fourier_basis(samples, first, band_count):
    sample_index = lax.broadcasted_iota(jnp.int32, (samples, band_count), 0)
    orders = lax.broadcasted_iota(jnp.int32, (samples, band_count), 1) + first
    phases = sample_index * orders % samples
    angles = phases.astype(jnp.float32) * (2.0 * math.pi / samples)
    return jnp.concatenate([jnp.cos(angles), -jnp.sin(angles)], axis=1) * (1.0 / math.sqrt(samples))

def owner_slots(owner_map):
    band_count = owner_map.shape[0]
    shared = owner_map[:, None] == owner_map[None, :]
    earlier = lax.broadcasted_iota(jnp.int32, (band_count, band_count), 1) < lax.broadcasted_iota(jnp.int32, (band_count, band_count), 0)
    return lax.optimization_barrier(jnp.sum((shared & earlier).astype(jnp.int32), axis=1)).astype(jnp.int32)

def merge_parts(real_own, imag_own, real_mirror, imag_mirror):
    power_own = real_own * real_own + imag_own * imag_own
    power_mirror = real_mirror * real_mirror + imag_mirror * imag_mirror
    total_power = power_own + power_mirror + WATER
    weight_own = (power_own + 0.5 * WATER) / total_power
    weight_mirror = (power_mirror + 0.5 * WATER) / total_power
    return (weight_own * real_own + weight_mirror * real_mirror, weight_own * imag_own + weight_mirror * imag_mirror)

def square_matrix(real_part, imag_part, factor):
    left_side = jnp.concatenate([real_part, imag_part], axis=1)
    right_side = jnp.concatenate([jnp.concatenate([real_part, imag_part], axis=1), jnp.concatenate([-imag_part, real_part], axis=1)], axis=0)
    result = jnp.dot(left_side, right_side, preferred_element_type=jnp.float32) * factor
    columns = real_part.shape[1]
    return jnp.stack([result[:, :columns], result[:, columns:]]).astype(jnp.bfloat16)

def reference(recorded, owner_map):
    fourier = fourier_basis(NT, FIRST, NF)
    spectrum = jnp.dot(recorded.reshape(S * R, NT), fourier, precision=lax.Precision.HIGHEST, preferred_element_type=jnp.float32).astype(jnp.bfloat16)
    band_major = spectrum.reshape(S, R, 2, NF).transpose(3, 2, 0, 1)
    factor = 1.0 / math.sqrt(R)

    def one_band(matrix):
        real_own = matrix[0].astype(jnp.float32)
        imag_own = matrix[1].astype(jnp.float32)
        real_merged, imag_merged = merge_parts(real_own, imag_own, real_own.T, imag_own.T)
        return square_matrix(real_merged.astype(jnp.bfloat16), imag_merged.astype(jnp.bfloat16), factor)
    band_squares = lax.map(one_band, band_major)
    slot_of = owner_slots(owner_map)
    result = jnp.zeros((NDEV, CAP, 2, S, R), jnp.bfloat16)
    return result.at[owner_map, slot_of].set(band_squares)
```

```python
import functools
import math

import jax
import jax.numpy as jnp
import numpy as np
from jax import lax
from jax.experimental import pallas as pl
from jax.experimental.pallas import tpu as pltpu
from jax.sharding import PartitionSpec as P

FIRST = 4
CAP = 2
WATER = 0.5
NT = 512
NF = 64
N = 1024
NDEV = 128
ROWS = 16
VMEM_LIMIT = 60 * 1024 * 1024


def basis_parts():
    t = np.arange(NT)[:, None]
    f = np.arange(NF)[None, :] + FIRST
    angles = 2.0 * math.pi * ((t * f) % NT) / NT
    both = np.stack([np.cos(angles), -np.sin(angles)], axis=2).reshape(NT, 2 * NF) / math.sqrt(NT)
    high = both.astype(jnp.bfloat16)
    low = (both - high.astype(np.float64)).astype(jnp.bfloat16)
    return np.concatenate([high, low], axis=1)


def spectrum_kernel(owner_ref, slot_ref, x_ref, basis_ref, out0, out1, wide, turned, spec, sems):
    step = pl.program_id(0)
    ch = 2 * NF
    x = x_ref[...].reshape(128 * ROWS, NT)
    high = x.astype(jnp.bfloat16)
    low = (x - high.astype(jnp.float32)).astype(jnp.bfloat16)
    first = jnp.dot(high, basis_ref[...], preferred_element_type=jnp.float32)
    second = jnp.dot(low, basis_ref[:, :ch], preferred_element_type=jnp.float32)
    wide[...] = first[:, :ch] + first[:, ch:] + second
    for r in range(ROWS):
        turned[pl.ds(r, ch, stride=ROWS), :] = wide[pl.ds(r, 128, stride=ROWS), :].T
    rows = turned[...].reshape(NF, 2, ROWS, 128).astype(jnp.bfloat16)
    spec[:, :, pl.ds(pl.multiple_of(step * ROWS, ROWS), ROWS), :] = rows

    @pl.when(step == pl.num_programs(0) - 1)
    def _():
        @pl.loop(0, NF)
        def _(f):
            owner = owner_ref[f]

            @pl.when(slot_ref[f] == 0)
            def _():
                pltpu.make_async_copy(spec.at[f], out0.at[owner], sems.at[f]).start()

            @pl.when(slot_ref[f] == 1)
            def _():
                pltpu.make_async_copy(spec.at[f], out1.at[owner], sems.at[f]).start()

        @pl.loop(0, NF)
        def _(f):
            pltpu.make_async_copy(spec.at[f], out0.at[0], sems.at[f]).wait()


def spectra_for_owners(recorded, owner_map, slot_of):
    tile = (NDEV, 2, 64, 128)
    return pl.pallas_call(
        spectrum_kernel,
        out_shape=[jax.ShapeDtypeStruct(tile, jnp.bfloat16)] * 2,
        grid_spec=pltpu.PrefetchScalarGridSpec(
            num_scalar_prefetch=2,
            grid=(64 // ROWS,),
            in_specs=[
                pl.BlockSpec((128, ROWS, NT), lambda i, *_: (0, i, 0)),
                pl.BlockSpec((NT, 4 * NF), lambda i, *_: (0, 0)),
            ],
            out_specs=[pl.BlockSpec(memory_space=pl.ANY)] * 2,
            scratch_shapes=[
                pltpu.VMEM((128 * ROWS, 128), jnp.float32),
                pltpu.VMEM((128 * ROWS, 128), jnp.float32),
                pltpu.VMEM((NF, 2, 64, 128), jnp.bfloat16),
                pltpu.SemaphoreType.DMA((NF,)),
            ],
        ),
        compiler_params=pltpu.CompilerParams(vmem_limit_bytes=VMEM_LIMIT),
        name="spectrum",
    )(owner_map, slot_of, recorded, jnp.asarray(basis_parts()))


def square_kernel(slot, owned_ref, got_ref, *refs):
    out, got, mat, res, sem_in, sems = refs[-6:]

    def blocks(fn):
        k = 0
        for col in range(4):
            for row in range(4):
                fn(row, col, k)
                k += 1

    def copy_out(row, col):
        r = pl.multiple_of(row * 256, 256)
        c = pl.multiple_of(col * 256, 256)
        return pltpu.make_async_copy(
            res.at[:, pl.ds(r, 256), pl.ds(c, 256)],
            out.at[0, slot, :, pl.ds(r, 256), pl.ds(c, 256)],
            sems.at[row * 4 + col],
        )

    @pl.when(owned_ref[slot] == 0)
    def _():
        res[...] = jnp.zeros_like(res)

        @pl.loop(0, 4)
        def _(row):
            @pl.loop(0, 4)
            def _(col):
                copy_out(row, col).start()

    @pl.when(owned_ref[slot] != 0)
    def _():
        load = pltpu.make_async_copy(got_ref, got, sem_in)
        load.start()
        load.wait()

        @pl.loop(0, 8)
        def _(b):
            @pl.loop(0, b + 1)
            def _(a):
                def block(row, col, c):
                    part = got[pl.ds(col * 16 + 2 * row, 2), c]
                    return part.reshape(128, 128).astype(jnp.float32)

                re_o, im_o = block(a, b, 0), block(a, b, 1)
                re_m, im_m = block(b, a, 0).T, block(b, a, 1).T
                p_o = re_o * re_o + im_o * im_o
                p_m = re_m * re_m + im_m * im_m
                inv = 1.0 / (p_o + p_m + WATER)
                w_o = (p_o + 0.5 * WATER) * inv
                w_m = (p_m + 0.5 * WATER) * inv
                ra = pl.multiple_of(a * 128, 128)
                rb = pl.multiple_of(b * 128, 128)
                for c, (own, mirror) in enumerate(((re_o, re_m), (im_o, im_m))):
                    merged = w_o * own + w_m * mirror
                    mat[c, pl.ds(ra, 128), pl.ds(rb, 128)] = merged.astype(jnp.bfloat16)
                    mat[c, pl.ds(rb, 128), pl.ds(ra, 128)] = merged.T.astype(jnp.bfloat16)

        @pl.loop(0, 4)
        def _(col):
            cc = pl.multiple_of(col * 256, 256)

            @pl.loop(0, col + 1)
            def _(row):
                rr = pl.multiple_of(row * 256, 256)

                def dot(left, right):
                    return jnp.dot(
                        mat[left, pl.ds(rr, 256), :],
                        mat[right, :, pl.ds(cc, 256)],
                        preferred_element_type=jnp.float32,
                    )

                factor = 1.0 / math.sqrt(N)
                real = (dot(0, 0) - dot(1, 1)) * factor
                imag = (dot(0, 1) + dot(1, 0)) * factor
                for c, part in enumerate((real, imag)):
                    res[c, pl.ds(rr, 256), pl.ds(cc, 256)] = part.astype(jnp.bfloat16)
                    res[c, pl.ds(cc, 256), pl.ds(rr, 256)] = part.T.astype(jnp.bfloat16)
                copy_out(row, col).start()

                @pl.when(row != col)
                def _():
                    copy_out(col, row).start()

    @pl.loop(0, 4)
    def _(row):
        @pl.loop(0, 4)
        def _(col):
            copy_out(row, col).wait()


def squares_of_slot(slot, owned, got, before):
    shape = (1, CAP, 2, N, N)
    inputs = [owned, got] + ([] if before is None else [before])
    return pl.pallas_call(
        functools.partial(square_kernel, slot),
        out_shape=jax.ShapeDtypeStruct(shape, jnp.bfloat16),
        grid_spec=pltpu.PrefetchScalarGridSpec(
            num_scalar_prefetch=1,
            grid=(),
            in_specs=[pl.BlockSpec(memory_space=pl.ANY)] * (len(inputs) - 1),
            out_specs=pl.BlockSpec(memory_space=pl.ANY),
            scratch_shapes=[
                pltpu.VMEM((NDEV, 2, 64, 128), jnp.bfloat16),
                pltpu.VMEM((2, N, N), jnp.bfloat16),
                pltpu.VMEM((2, N, N), jnp.bfloat16),
                pltpu.SemaphoreType.DMA,
                pltpu.SemaphoreType.DMA((16,)),
            ],
        ),
        compiler_params=pltpu.CompilerParams(vmem_limit_bytes=VMEM_LIMIT),
        input_output_aliases={} if before is None else {2: 0},
        cost_estimate=pl.CostEstimate(flops=8 * N**3, bytes_accessed=8 * N * N, transcendentals=0),
        name=f"squares{slot}",
    )(*inputs)


def shards(recorded, owner_map):
    shared = owner_map[:, None] == owner_map[None, :]
    earlier = lax.broadcasted_iota(jnp.int32, (NF, NF), 1) < lax.broadcasted_iota(jnp.int32, (NF, NF), 0)
    slot_of = jnp.sum((shared & earlier).astype(jnp.int32), axis=1)
    me = lax.axis_index("src") * lax.axis_size("rcv") + lax.axis_index("rcv")
    mine = jnp.sum((owner_map == me).astype(jnp.int32))
    owned = (mine > jnp.arange(CAP, dtype=jnp.int32)).astype(jnp.int32)
    sent = spectra_for_owners(recorded, owner_map, slot_of)
    got = [lax.all_to_all(part, ("src", "rcv"), split_axis=0, concat_axis=0, tiled=True) for part in sent]
    result = squares_of_slot(0, owned, got[0], None)
    return squares_of_slot(1, owned, got[1], result)


def solution(mesh):
    in_specs = (P("src", "rcv", None), P())
    out_specs = P(("src", "rcv"), None, None, None, None)
    return jax.shard_map(shards, mesh=mesh, in_specs=in_specs, out_specs=out_specs, check_vma=False)
```

```python
import functools
import math

import jax
import jax.numpy as jnp
import numpy as np
from jax import lax
from jax.experimental import pallas as pl
from jax.experimental.pallas import tpu as pltpu
from jax.sharding import PartitionSpec as P

FIRST = 4
CAP = 2
WATER = 0.5
NT = 512
NF = 64
N = 1024
NDEV = 128
TILES = NDEV + 8
CHUNK = 16
STEPS = 64 // CHUNK
VMEM_LIMIT = 62 * 1024 * 1024
MESH = pl.DeviceIdType.MESH


def basis_parts():
    t = np.arange(NT)[:, None]
    f = np.arange(NF)[None, :] + FIRST
    angles = 2.0 * math.pi * ((t * f) % NT) / NT
    both = np.concatenate([np.cos(angles), -np.sin(angles)], axis=1) / math.sqrt(NT)
    high = both.astype(jnp.bfloat16)
    low = (both - high.astype(np.float64)).astype(jnp.bfloat16)
    return np.concatenate([high, low], axis=1)


def merge(own, mirror):
    def power(v):
        square = v * v
        return square + pltpu.roll(square, 64, axis=square.ndim - 1)

    p_own, p_mirror = power(own), power(mirror)
    inv = 1.0 / (p_own + p_mirror + WATER)
    return ((p_own + 0.5 * WATER) * own + (p_mirror + 0.5 * WATER) * mirror) * inv


def peer(k, x, y, z, c):
    dx = k % 4
    dy = (k // 4 + dx) % 4
    dz = (k // 16 + dy) % 4
    xs, ys, zs, cs = (x + dx) % 4, (y + dy) % 4, (z + dz) % 4, (c + k // 64) % 2
    return ys * 2 + cs, xs * 4 + zs


def exchange_kernel(
    table, x_hbm, basis_ref, got0, got1,
    xa, xb, wide, turned, kept, sent, mirror, select, extra,
    load_a, load_b, send_m, recv_m, send_o, recv_o, send_e, own_sem,
):
    i, q = lax.axis_index("src"), lax.axis_index("rcv")
    y, c = i // 2, i % 2
    x, z = q // 4, q % 4
    me = i * 16 + q
    first = q == 2 * i
    second = q == 2 * i + 1
    keep = jnp.where(q > 2 * i + 1, 1 - q % 2, jnp.where(q < 2 * i, q % 2, 0))
    away = 1 - keep
    got = (got0, got1)

    barrier = pltpu.get_barrier_semaphore()

    @pl.loop(1, NDEV)
    def _(k):
        pl.semaphore_signal(barrier, inc=1, device_id=peer(k, x, y, z, c), device_id_type=MESH)

    def fetch_a(k):
        src = x_hbm.at[pl.ds(64 * away + CHUNK * k, CHUNK)]
        return pltpu.make_async_copy(src, xa.at[k % 2], load_a.at[k % 2])

    def fetch_b(k):
        src = x_hbm.at[pl.ds(64 * keep, 64), pl.ds(CHUNK * k, CHUNK)]
        return pltpu.make_async_copy(src, xb.at[k % 2], load_b.at[k % 2])

    for k in range(2):
        fetch_a(k).start()
    for k in range(2):
        fetch_b(k).start()

    ch = 2 * NF

    def transform(values):
        high = values.astype(jnp.bfloat16)
        low = (values - high.astype(jnp.float32)).astype(jnp.bfloat16)
        one = jnp.dot(high, basis_ref[...], preferred_element_type=jnp.float32)
        two = jnp.dot(low, basis_ref[:, :ch], preferred_element_type=jnp.float32)
        wide[...] = one[:, :ch] + one[:, ch:] + two

    def turn(rows_of, k, out):
        low_half = lax.broadcasted_iota(jnp.int32, (NF, 128), 1) < 64
        for j in range(CHUNK // 2):
            both = rows_of(j).T
            real, imag = both[:NF], both[NF:]
            turned[pl.ds(2 * j, NF, stride=CHUNK), :] = jnp.where(low_half, real, pltpu.roll(imag, 64, axis=1))
            turned[pl.ds(2 * j + 1, NF, stride=CHUNK), :] = jnp.where(low_half, pltpu.roll(real, 64, axis=1), imag)
        rows = pl.ds(pl.multiple_of(k * CHUNK, CHUNK), CHUNK)
        out[:, rows, :] = turned[...].reshape(NF, CHUNK, 128).astype(jnp.bfloat16)

    def mirror_copy(k):
        rows = pl.ds(pl.multiple_of(k * CHUNK, CHUNK), CHUNK)
        return pltpu.make_async_remote_copy(
            src_ref=sent.at[:, rows, :],
            dst_ref=mirror.at[:, rows, :],
            send_sem=send_m.at[k],
            recv_sem=recv_m.at[k],
            device_id=(q // 2, 2 * i + away),
            device_id_type=MESH,
        )

    @pl.loop(0, STEPS)
    def _(k):
        fetch_a(k).wait()
        transform(xa[k % 2].reshape(CHUNK * 64, NT))

        @pl.when(k + 2 < STEPS)
        def _():
            fetch_a(k + 2).start()

        turn(lambda j: wide[pl.ds(128 * j, 128), :], k, sent)

        @pl.when(k == 0)
        def _():
            pl.semaphore_wait(barrier, NDEV - 1)

        @pl.when(jnp.logical_not(second))
        def _():
            mirror_copy(k).start()

    def strided(j):
        parts = [wide[pl.ds(2 * j + h, 64, stride=CHUNK), :] for h in range(2)]
        return jnp.concatenate(parts, axis=0)

    @pl.loop(0, STEPS)
    def _(k):
        fetch_b(k).wait()
        transform(xb[k % 2].reshape(CHUNK * 64, NT))

        @pl.when(k + 2 < STEPS)
        def _():
            fetch_b(k + 2).start()

        turn(strided, k, kept)

    @pl.when(jnp.logical_not(first))
    def _():
        @pl.loop(0, STEPS)
        def _(k):
            mirror_copy(k).wait_recv()
            rows = pl.ds(pl.multiple_of(k * CHUNK, CHUNK), CHUNK)

            @pl.loop(0, NF // 4)
            def _(f):
                own = kept[pl.ds(f * 4, 4), rows, :].astype(jnp.float32)
                other = mirror[pl.ds(f * 4, 4), rows, :].astype(jnp.float32)
                kept[pl.ds(f * 4, 4), rows, :] = merge(own, other).astype(jnp.bfloat16)

    def extra_copy(slot, k):
        device = peer(k, x, y, z, c)
        return pltpu.make_async_remote_copy(
            src_ref=extra.at[slot, device[0] * 16 + device[1]],
            dst_ref=got[slot].at[NDEV + i],
            send_sem=send_e.at[slot],
            recv_sem=recv_o.at[slot],
            device_id=device,
            device_id_type=MESH,
        )

    def owner_copy(slot, k):
        device = peer(k, x, y, z, c)
        return pltpu.make_async_remote_copy(
            src_ref=select.at[slot, device[0] * 16 + device[1]],
            dst_ref=got[slot].at[me],
            send_sem=send_o.at[slot],
            recv_sem=recv_o.at[slot],
            device_id=device,
            device_id_type=MESH,
        )

    def local_copies(slot):
        own = pltpu.make_async_copy(select.at[slot, me], got[slot].at[me], own_sem.at[slot])
        more = pltpu.make_async_copy(extra.at[slot, me], got[slot].at[NDEV + i], own_sem.at[2 + slot])
        return own, more

    for slot in range(CAP):
        @pl.loop(0, NDEV)
        def _(d):
            select[slot, d] = kept[table[slot, d]]

        @pl.when(second)
        def _():
            @pl.loop(0, NDEV)
            def _(d):
                extra[slot, d] = sent[table[slot, d]]

    for slot in range(CAP):
        own, more = local_copies(slot)
        own.start()

        @pl.when(jnp.logical_not(second))
        def _():
            @pl.loop(1, NDEV)
            def _(k):
                owner_copy(slot, k).start()

        @pl.when(second)
        def _():
            more.start()

            @pl.loop(1, NDEV)
            def _(k):
                owner_copy(slot, k).start()
                extra_copy(slot, k).start()

    @pl.when(jnp.logical_not(second))
    def _():
        @pl.loop(0, STEPS)
        def _(k):
            mirror_copy(k).wait_send()

    for slot in range(CAP):
        own, more = local_copies(slot)
        own.wait()
        most = select.at[slot, pl.ds(0, NDEV - 1)]
        pltpu.make_async_copy(most, most, send_o.at[slot]).wait()

        def arrived(count):
            part = got[slot].at[pl.ds(0, count)]
            pltpu.make_async_copy(part, part, recv_o.at[slot]).wait()

        @pl.when(second)
        def _():
            more.wait()
            pltpu.make_async_copy(most, most, send_e.at[slot]).wait()
            arrived(TILES - 2)

        @pl.when(jnp.logical_not(second))
        def _():
            arrived(TILES - 1)


def tiles_at_owners(recorded, table):
    tile = (64, 128)
    dma = pltpu.SemaphoreType.DMA
    return pl.pallas_call(
        exchange_kernel,
        out_shape=[jax.ShapeDtypeStruct((TILES,) + tile, jnp.bfloat16)] * 2,
        in_specs=[
            pl.BlockSpec(memory_space=pltpu.SMEM),
            pl.BlockSpec(memory_space=pl.ANY),
            pl.BlockSpec(memory_space=pltpu.VMEM),
        ],
        out_specs=[pl.BlockSpec(memory_space=pl.ANY)] * 2,
        scratch_shapes=[
            pltpu.VMEM((2, CHUNK, 64, NT), jnp.float32),
            pltpu.VMEM((2, 64, CHUNK, NT), jnp.float32),
            pltpu.VMEM((CHUNK * 64, 2 * NF), jnp.float32),
            pltpu.VMEM((NF * CHUNK, 128), jnp.float32),
            pltpu.VMEM((NF,) + tile, jnp.bfloat16),
            pltpu.VMEM((NF,) + tile, jnp.bfloat16),
            pltpu.VMEM((NF,) + tile, jnp.bfloat16),
            pltpu.VMEM((CAP, NDEV) + tile, jnp.bfloat16),
            pltpu.VMEM((CAP, NDEV) + tile, jnp.bfloat16),
            dma((2,)), dma((2,)), dma((STEPS,)), dma((STEPS,)),
            dma((CAP,)), dma((CAP,)), dma((CAP,)), dma((2 * CAP,)),
        ],
        compiler_params=pltpu.CompilerParams(
            vmem_limit_bytes=VMEM_LIMIT, collective_id=0, has_side_effects=True
        ),
        name="exchange",
    )(table, recorded, jnp.asarray(basis_parts()))


def square_kernel(owned_ref, got0, got1, out, got, mat, res, sem_in, sems):
    for slot in range(CAP):
        @pl.when(owned_ref[slot] != 0)
        def _():
            pltpu.make_async_copy((got0, got1)[slot], got.at[slot], sem_in.at[slot]).start()

    def copy_out(slot, row, col):
        r = pl.multiple_of(row * 256, 256)
        c = pl.multiple_of(col * 256, 256)
        return pltpu.make_async_copy(
            res.at[slot, :, pl.ds(r, 256), pl.ds(c, 256)],
            out.at[0, slot, :, pl.ds(r, 256), pl.ds(c, 256)],
            sems.at[slot * 16 + row * 4 + col],
        )

    low = lax.broadcasted_iota(jnp.int32, (64, 128), 1) < 64

    def swap(v):
        return pltpu.roll(v, 64, axis=1)

    def put(a, b, top, bottom):
        ra = pl.multiple_of(a * 128, 128)
        rb = pl.multiple_of(b * 128, 128)
        for c in range(2):
            block = jnp.concatenate([top[c], bottom[c]], axis=0)
            mat[c, pl.ds(ra, 128), pl.ds(rb, 128)] = block.astype(jnp.bfloat16)
            mat[c, pl.ds(rb, 128), pl.ds(ra, 128)] = block.T.astype(jnp.bfloat16)

    @pl.loop(0, CAP)
    def _(slot):
        @pl.when(owned_ref[slot] == 0)
        def _():
            res[slot] = jnp.zeros((2, N, N), jnp.bfloat16)

            @pl.loop(0, 4)
            def _(row):
                @pl.loop(0, 4)
                def _(col):
                    copy_out(slot, row, col).start()

        @pl.when(owned_ref[slot] != 0)
        def _():
            pltpu.make_async_copy(got0, got.at[slot], sem_in.at[slot]).wait()

            def tile(k):
                return got[slot, k].astype(jnp.float32)

            @pl.loop(0, 8)
            def _(b):
                @pl.loop(0, b)
                def _(a):
                    t00, t11 = tile(b * 16 + 2 * a), tile(b * 16 + 2 * a + 1)
                    u01, u10 = tile(a * 16 + 2 * b + 1), tile(a * 16 + 2 * b)
                    both = jnp.concatenate([u01, u10], axis=0).T
                    real, imag = swap(both[:64]), swap(both[64:])
                    top = (jnp.where(low, t00, real), jnp.where(low, swap(t00), imag))
                    bottom = (jnp.where(low, real, swap(t11)), jnp.where(low, imag, t11))
                    put(a, b, top, bottom)

                d0, d1, u = tile(b * 16 + 2 * b), tile(NDEV + b), tile(b * 16 + 2 * b + 1)
                both = jnp.concatenate([d0, d1], axis=0).T
                d0 = merge(d0, jnp.where(low, both[:64], swap(both[64:])))
                d1 = merge(d1, jnp.where(low, swap(both[:64]), both[64:]))
                other = jnp.concatenate([u, u], axis=0).T
                top = (jnp.where(low, d0, other[:64]), jnp.where(low, swap(d0), other[64:]))
                bottom = (jnp.where(low, u, swap(d1)), jnp.where(low, swap(u), d1))
                put(b, b, top, bottom)

            @pl.loop(0, 4)
            def _(col):
                cc = pl.multiple_of(col * 256, 256)

                @pl.loop(0, col + 1)
                def _(row):
                    rr = pl.multiple_of(row * 256, 256)

                    def dot(left, right):
                        return jnp.dot(
                            mat[left, pl.ds(rr, 256), :],
                            mat[right, :, pl.ds(cc, 256)],
                            preferred_element_type=jnp.float32,
                        )

                    factor = 1.0 / math.sqrt(N)
                    real = (dot(0, 0) - dot(1, 1)) * factor
                    imag = (dot(0, 1) + dot(1, 0)) * factor
                    for c, part in enumerate((real, imag)):
                        res[slot, c, pl.ds(rr, 256), pl.ds(cc, 256)] = part.astype(jnp.bfloat16)
                        res[slot, c, pl.ds(cc, 256), pl.ds(rr, 256)] = part.T.astype(jnp.bfloat16)
                    copy_out(slot, row, col).start()

                    @pl.when(row != col)
                    def _():
                        copy_out(slot, col, row).start()

    @pl.loop(0, CAP)
    def _(slot):
        @pl.loop(0, 4)
        def _(row):
            @pl.loop(0, 4)
            def _(col):
                copy_out(slot, row, col).wait()


def squares_of(owned, got0, got1):
    return pl.pallas_call(
        square_kernel,
        out_shape=jax.ShapeDtypeStruct((1, CAP, 2, N, N), jnp.bfloat16),
        in_specs=[pl.BlockSpec(memory_space=pltpu.SMEM)] + [pl.BlockSpec(memory_space=pl.ANY)] * 2,
        out_specs=pl.BlockSpec(memory_space=pl.ANY),
        scratch_shapes=[
            pltpu.VMEM((CAP, TILES, 64, 128), jnp.bfloat16),
            pltpu.VMEM((2, N, N), jnp.bfloat16),
            pltpu.VMEM((CAP, 2, N, N), jnp.bfloat16),
            pltpu.SemaphoreType.DMA((CAP,)),
            pltpu.SemaphoreType.DMA((CAP * 16,)),
        ],
        compiler_params=pltpu.CompilerParams(vmem_limit_bytes=VMEM_LIMIT),
        name="squares",
    )(owned, got0, got1)


def shards(recorded, owner_map):
    bands = jnp.arange(NF, dtype=jnp.int32)
    shared = owner_map[:, None] == owner_map[None, :]
    slot_of = jnp.sum((shared & (bands[None, :] < bands[:, None])).astype(jnp.int32), axis=1)
    places = jnp.arange(CAP * NDEV, dtype=jnp.int32).reshape(CAP, NDEV)
    hit = (slot_of * NDEV + owner_map)[None, None, :] == places[:, :, None]
    table = jnp.sum(jnp.where(hit, bands[None, None, :], 0), axis=2)
    me = lax.axis_index("src") * lax.axis_size("rcv") + lax.axis_index("rcv")
    mine = jnp.sum((owner_map == me).astype(jnp.int32))
    owned = (mine > jnp.arange(CAP, dtype=jnp.int32)).astype(jnp.int32)
    got0, got1 = tiles_at_owners(recorded, table)
    return squares_of(owned, got0, got1)


def solution(mesh):
    in_specs = (P("src", "rcv", None), P())
    out_specs = P(("src", "rcv"), None, None, None, None)
    return jax.shard_map(shards, mesh=mesh, in_specs=in_specs, out_specs=out_specs, check_vma=False)
```

```python
import functools
import math

import jax
import jax.numpy as jnp
import numpy as np
from jax import lax
from jax.experimental import pallas as pl
from jax.experimental.pallas import tpu as pltpu
from jax.sharding import PartitionSpec as P

FIRST = 4
CAP = 2
WATER = 0.5
NT = 512
NF = 64
N = 1024
NDEV = 128
TILES = NDEV + 8
CHUNK = 16
STEPS = 64 // CHUNK
VMEM_LIMIT = 62 * 1024 * 1024
MESH = pl.DeviceIdType.MESH


def basis_parts():
    t = np.arange(NT)[:, None]
    f = np.arange(NF)[None, :] + FIRST
    angles = 2.0 * math.pi * ((t * f) % NT) / NT
    both = np.concatenate([np.cos(angles), -np.sin(angles)], axis=1) / math.sqrt(NT)
    high = both.astype(jnp.bfloat16)
    low = (both - high.astype(np.float64)).astype(jnp.bfloat16)
    return np.concatenate([high, low], axis=1)


def merge(own, mirror):
    def power(v):
        square = v * v
        return square + pltpu.roll(square, 64, axis=square.ndim - 1)

    p_own, p_mirror = power(own), power(mirror)
    inv = 1.0 / (p_own + p_mirror + WATER)
    return ((p_own + 0.5 * WATER) * own + (p_mirror + 0.5 * WATER) * mirror) * inv


def peer(k, x, y, z, c):
    dx = k % 4
    dy = (k // 4 + dx) % 4
    dz = (k // 16 + dy) % 4
    xs, ys, zs, cs = (x + dx) % 4, (y + dy) % 4, (z + dz) % 4, (c + k // 64) % 2
    return ys * 2 + cs, xs * 4 + zs


def away_half(i, q):
    return jnp.where(q > 2 * i + 1, q % 2, jnp.where(q < 2 * i, 1 - q % 2, 1))


def exchange_kernel(
    table, x_hbm, basis_ref, got0, got1,
    xa, xb, wide, turned, kept, sent, mirror, relay, select, extra,
    load_a, load_b, send_m, recv_m, send_r, recv_r, send_o, recv_o, send_e, own_sem,
):
    i, q = lax.axis_index("src"), lax.axis_index("rcv")
    y, c = i // 2, i % 2
    x, z = q // 4, q % 4
    me = i * 16 + q
    first = q == 2 * i
    second = q == 2 * i + 1
    far = (x + 2) % 4 == y
    away = away_half(i, q)
    keep = 1 - away
    got = (got0, got1)

    barrier = pltpu.get_barrier_semaphore()

    @pl.loop(1, NDEV)
    def _(k):
        pl.semaphore_signal(barrier, inc=1, device_id=peer(k, x, y, z, c), device_id_type=MESH)

    def fetch_a(k):
        src = x_hbm.at[pl.ds(64 * away + CHUNK * k, CHUNK)]
        return pltpu.make_async_copy(src, xa.at[k % 2], load_a.at[k % 2])

    def fetch_b(k):
        src = x_hbm.at[pl.ds(64 * keep, 64), pl.ds(CHUNK * k, CHUNK)]
        return pltpu.make_async_copy(src, xb.at[k % 2], load_b.at[k % 2])

    for k in range(2):
        fetch_a(k).start()
    for k in range(2):
        fetch_b(k).start()

    ch = 2 * NF

    def transform(values):
        high = values.astype(jnp.bfloat16)
        low = (values - high.astype(jnp.float32)).astype(jnp.bfloat16)
        one = jnp.dot(high, basis_ref[...], preferred_element_type=jnp.float32)
        two = jnp.dot(low, basis_ref[:, :ch], preferred_element_type=jnp.float32)
        wide[...] = one[:, :ch] + one[:, ch:] + two

    def turn(rows_of, k, out):
        low_half = lax.broadcasted_iota(jnp.int32, (NF, 128), 1) < 64
        for j in range(CHUNK // 2):
            both = rows_of(j).T
            real, imag = both[:NF], both[NF:]
            turned[pl.ds(2 * j, NF, stride=CHUNK), :] = jnp.where(low_half, real, pltpu.roll(imag, 64, axis=1))
            turned[pl.ds(2 * j + 1, NF, stride=CHUNK), :] = jnp.where(low_half, pltpu.roll(real, 64, axis=1), imag)
        rows = pl.ds(pl.multiple_of(k * CHUNK, CHUNK), CHUNK)
        out[:, rows, :] = turned[...].reshape(NF, CHUNK, 128).astype(jnp.bfloat16)

    def mirror_copy(k):
        rows = pl.ds(pl.multiple_of(k * CHUNK, CHUNK), CHUNK)
        return pltpu.make_async_remote_copy(
            src_ref=sent.at[:, rows, :],
            dst_ref=mirror.at[:, rows, :],
            send_sem=send_m.at[k],
            recv_sem=recv_m.at[k],
            device_id=(q // 2, 2 * i + away),
            device_id_type=MESH,
        )

    def chunk_of(ref, k):
        return ref.at[:, pl.ds(pl.multiple_of(k * CHUNK, CHUNK), CHUNK), :]

    def relay_in(k):
        step = 1 + 2 * (k % 2)
        xs, ys = (x + step) % 4, (y + step) % 4
        return pltpu.make_async_remote_copy(
            src_ref=chunk_of(sent, k),
            dst_ref=relay.at[k],
            send_sem=send_m.at[k],
            recv_sem=recv_r.at[k],
            device_id=(ys * 2 + c, xs * 4 + z),
            device_id_type=MESH,
        )

    def relay_out(k):
        step = 3 - 2 * (k % 2)
        i_from, q_from = ((y + step) % 4) * 2 + c, ((x + step) % 4) * 4 + z
        return pltpu.make_async_remote_copy(
            src_ref=relay.at[k],
            dst_ref=chunk_of(mirror, k),
            send_sem=send_r.at[k],
            recv_sem=recv_m.at[k],
            device_id=(q_from // 2, 2 * i_from + away_half(i_from, q_from)),
            device_id_type=MESH,
        )

    near = jnp.logical_not(jnp.logical_or(second, far))

    @pl.loop(0, STEPS)
    def _(k):
        fetch_a(k).wait()
        transform(xa[k % 2].reshape(CHUNK * 64, NT))

        @pl.when(k + 2 < STEPS)
        def _():
            fetch_a(k + 2).start()

        turn(lambda j: wide[pl.ds(128 * j, 128), :], k, sent)

        @pl.when(k == 0)
        def _():
            pl.semaphore_wait(barrier, NDEV - 1)

        @pl.when(near)
        def _():
            mirror_copy(k).start()

        @pl.when(far)
        def _():
            relay_in(k).start()

    def strided(j):
        parts = [wide[pl.ds(2 * j + h, 64, stride=CHUNK), :] for h in range(2)]
        return jnp.concatenate(parts, axis=0)

    @pl.loop(0, STEPS)
    def _(k):
        fetch_b(k).wait()
        transform(xb[k % 2].reshape(CHUNK * 64, NT))

        @pl.when(k + 2 < STEPS)
        def _():
            fetch_b(k + 2).start()

        turn(strided, k, kept)

        @pl.when(far)
        def _():
            relay_in(k).wait_recv()
            relay_out(k).start()

    @pl.when(jnp.logical_not(first))
    def _():
        @pl.loop(0, STEPS)
        def _(k):
            mirror_copy(k).wait_recv()
            rows = pl.ds(pl.multiple_of(k * CHUNK, CHUNK), CHUNK)

            @pl.loop(0, NF // 4)
            def _(f):
                own = kept[pl.ds(f * 4, 4), rows, :].astype(jnp.float32)
                other = mirror[pl.ds(f * 4, 4), rows, :].astype(jnp.float32)
                kept[pl.ds(f * 4, 4), rows, :] = merge(own, other).astype(jnp.bfloat16)

    def extra_copy(slot, k):
        device = peer(k, x, y, z, c)
        return pltpu.make_async_remote_copy(
            src_ref=extra.at[slot, device[0] * 16 + device[1]],
            dst_ref=got[slot].at[NDEV + i],
            send_sem=send_e.at[slot],
            recv_sem=recv_o.at[slot],
            device_id=device,
            device_id_type=MESH,
        )

    def owner_copy(slot, k):
        device = peer(k, x, y, z, c)
        return pltpu.make_async_remote_copy(
            src_ref=select.at[slot, device[0] * 16 + device[1]],
            dst_ref=got[slot].at[me],
            send_sem=send_o.at[slot],
            recv_sem=recv_o.at[slot],
            device_id=device,
            device_id_type=MESH,
        )

    def local_copies(slot):
        own = pltpu.make_async_copy(select.at[slot, me], got[slot].at[me], own_sem.at[slot])
        more = pltpu.make_async_copy(extra.at[slot, me], got[slot].at[NDEV + i], own_sem.at[2 + slot])
        return own, more

    for slot in range(CAP):
        @pl.loop(0, NDEV)
        def _(d):
            select[slot, d] = kept[table[slot, d]]

        @pl.when(second)
        def _():
            @pl.loop(0, NDEV)
            def _(d):
                extra[slot, d] = sent[table[slot, d]]

    for slot in range(CAP):
        own, more = local_copies(slot)
        own.start()

        @pl.when(jnp.logical_not(second))
        def _():
            @pl.loop(1, NDEV)
            def _(k):
                owner_copy(slot, k).start()

        @pl.when(second)
        def _():
            more.start()

            @pl.loop(1, NDEV)
            def _(k):
                owner_copy(slot, k).start()
                extra_copy(slot, k).start()

    @pl.when(near)
    def _():
        @pl.loop(0, STEPS)
        def _(k):
            mirror_copy(k).wait_send()

    @pl.when(far)
    def _():
        @pl.loop(0, STEPS)
        def _(k):
            relay_in(k).wait_send()
            relay_out(k).wait_send()

    for slot in range(CAP):
        own, more = local_copies(slot)
        own.wait()
        most = select.at[slot, pl.ds(0, NDEV - 1)]
        pltpu.make_async_copy(most, most, send_o.at[slot]).wait()

        def arrived(count):
            part = got[slot].at[pl.ds(0, count)]
            pltpu.make_async_copy(part, part, recv_o.at[slot]).wait()

        @pl.when(second)
        def _():
            more.wait()
            pltpu.make_async_copy(most, most, send_e.at[slot]).wait()
            arrived(TILES - 2)

        @pl.when(jnp.logical_not(second))
        def _():
            arrived(TILES - 1)


def tiles_at_owners(recorded, table):
    tile = (64, 128)
    dma = pltpu.SemaphoreType.DMA
    return pl.pallas_call(
        exchange_kernel,
        out_shape=[jax.ShapeDtypeStruct((TILES,) + tile, jnp.bfloat16)] * 2,
        in_specs=[
            pl.BlockSpec(memory_space=pltpu.SMEM),
            pl.BlockSpec(memory_space=pl.ANY),
            pl.BlockSpec(memory_space=pltpu.VMEM),
        ],
        out_specs=[pl.BlockSpec(memory_space=pl.ANY)] * 2,
        scratch_shapes=[
            pltpu.VMEM((2, CHUNK, 64, NT), jnp.float32),
            pltpu.VMEM((2, 64, CHUNK, NT), jnp.float32),
            pltpu.VMEM((CHUNK * 64, 2 * NF), jnp.float32),
            pltpu.VMEM((NF * CHUNK, 128), jnp.float32),
            pltpu.VMEM((NF,) + tile, jnp.bfloat16),
            pltpu.VMEM((NF,) + tile, jnp.bfloat16),
            pltpu.VMEM((NF,) + tile, jnp.bfloat16),
            pltpu.VMEM((STEPS, NF, CHUNK, 128), jnp.bfloat16),
            pltpu.VMEM((CAP, NDEV) + tile, jnp.bfloat16),
            pltpu.VMEM((CAP, NDEV) + tile, jnp.bfloat16),
            dma((2,)), dma((2,)), dma((STEPS,)), dma((STEPS,)), dma((STEPS,)), dma((STEPS,)),
            dma((CAP,)), dma((CAP,)), dma((CAP,)), dma((2 * CAP,)),
        ],
        compiler_params=pltpu.CompilerParams(
            vmem_limit_bytes=VMEM_LIMIT, collective_id=0, has_side_effects=True
        ),
        name="exchange",
    )(table, recorded, jnp.asarray(basis_parts()))


def square_kernel(owner_ref, got0, got1, out, owned_ref, got, mat, res, sem_in, sems):
    me = lax.axis_index("src") * 16 + lax.axis_index("rcv")
    mine = lax.fori_loop(0, NF, lambda f, n: n + jnp.where(owner_ref[f] == me, 1, 0), 0)
    for slot in range(CAP):
        owned_ref[slot] = jnp.where(mine > slot, 1, 0)

    for slot in range(CAP):
        @pl.when(owned_ref[slot] != 0)
        def _():
            pltpu.make_async_copy((got0, got1)[slot], got.at[slot], sem_in.at[slot]).start()

    def copy_out(slot, row, col):
        r = pl.multiple_of(row * 256, 256)
        c = pl.multiple_of(col * 256, 256)
        return pltpu.make_async_copy(
            res.at[slot, :, pl.ds(r, 256), pl.ds(c, 256)],
            out.at[0, slot, :, pl.ds(r, 256), pl.ds(c, 256)],
            sems.at[slot * 16 + row * 4 + col],
        )

    low = lax.broadcasted_iota(jnp.int32, (64, 128), 1) < 64

    def swap(v):
        return pltpu.roll(v, 64, axis=1)

    def put(a, b, top, bottom):
        ra = pl.multiple_of(a * 128, 128)
        rb = pl.multiple_of(b * 128, 128)
        for c in range(2):
            mat[c, pl.ds(ra, 64), pl.ds(rb, 128)] = top[c].astype(jnp.bfloat16)
            mat[c, pl.ds(ra + 64, 64), pl.ds(rb, 128)] = bottom[c].astype(jnp.bfloat16)

    @pl.loop(0, CAP)
    def _(slot):
        @pl.when(owned_ref[slot] == 0)
        def _():
            res[slot] = jnp.zeros((2, N, N), jnp.bfloat16)

            @pl.loop(0, 4)
            def _(row):
                @pl.loop(0, 4)
                def _(col):
                    copy_out(slot, row, col).start()

        @pl.when(owned_ref[slot] != 0)
        def _():
            pltpu.make_async_copy(got0, got.at[slot], sem_in.at[slot]).wait()

            def tile(k):
                return got[slot, k].astype(jnp.float32)

            def pair(a, b):
                t00, t11 = tile(b * 16 + 2 * a), tile(b * 16 + 2 * a + 1)
                u01, u10 = tile(a * 16 + 2 * b + 1), tile(a * 16 + 2 * b)
                turned = jnp.concatenate([u01, u10], axis=0).T
                real, imag = swap(turned[:64]), swap(turned[64:])
                top = (jnp.where(low, t00, real), jnp.where(low, swap(t00), imag))
                bottom = (jnp.where(low, real, swap(t11)), jnp.where(low, imag, t11))
                put(a, b, top, bottom)
                turned = jnp.concatenate([t00, t11], axis=0).T
                real, imag = turned[:64], turned[64:]
                top = (jnp.where(low, real, swap(u10)), jnp.where(low, imag, u10))
                bottom = (jnp.where(low, u01, real), jnp.where(low, swap(u01), imag))
                put(b, a, top, bottom)

            def diagonal(b):
                d0, d1, u = tile(b * 16 + 2 * b), tile(NDEV + b), tile(b * 16 + 2 * b + 1)
                both = jnp.concatenate([d0, d1], axis=0).T
                d0 = merge(d0, jnp.where(low, both[:64], swap(both[64:])))
                d1 = merge(d1, jnp.where(low, swap(both[:64]), both[64:]))
                other = jnp.concatenate([u, u], axis=0).T
                top = (jnp.where(low, d0, other[:64]), jnp.where(low, swap(d0), other[64:]))
                bottom = (jnp.where(low, u, swap(d1)), jnp.where(low, swap(u), d1))
                put(b, b, top, bottom)

            @pl.loop(0, 7)
            def _(k):
                pair(k, 7)
                for j in range(1, 4):
                    one, two = (k + j) % 7, (k + 7 - j) % 7
                    pair(jnp.minimum(one, two), jnp.maximum(one, two))

            @pl.loop(0, 4)
            def _(b):
                diagonal(2 * b)
                diagonal(2 * b + 1)

            @pl.loop(0, 4)
            def _(col):
                cc = pl.multiple_of(col * 256, 256)

                @pl.loop(0, col + 1)
                def _(row):
                    rr = pl.multiple_of(row * 256, 256)

                    def dot(left, right):
                        return jnp.dot(
                            mat[left, pl.ds(rr, 256), :],
                            mat[right, :, pl.ds(cc, 256)],
                            preferred_element_type=jnp.float32,
                        )

                    factor = 1.0 / math.sqrt(N)
                    real = (dot(0, 0) - dot(1, 1)) * factor
                    imag = (dot(0, 1) + dot(1, 0)) * factor
                    for c, part in enumerate((real, imag)):
                        res[slot, c, pl.ds(rr, 256), pl.ds(cc, 256)] = part.astype(jnp.bfloat16)
                        res[slot, c, pl.ds(cc, 256), pl.ds(rr, 256)] = part.T.astype(jnp.bfloat16)
                    copy_out(slot, row, col).start()

                    @pl.when(row != col)
                    def _():
                        copy_out(slot, col, row).start()

    @pl.loop(0, CAP)
    def _(slot):
        @pl.loop(0, 4)
        def _(row):
            @pl.loop(0, 4)
            def _(col):
                copy_out(slot, row, col).wait()


def squares_of(owner_map, got0, got1):
    return pl.pallas_call(
        square_kernel,
        out_shape=jax.ShapeDtypeStruct((1, CAP, 2, N, N), jnp.bfloat16),
        in_specs=[pl.BlockSpec(memory_space=pltpu.SMEM)] + [pl.BlockSpec(memory_space=pl.ANY)] * 2,
        out_specs=pl.BlockSpec(memory_space=pl.ANY),
        scratch_shapes=[
            pltpu.SMEM((CAP,), jnp.int32),
            pltpu.VMEM((CAP, TILES, 64, 128), jnp.bfloat16),
            pltpu.VMEM((2, N, N), jnp.bfloat16),
            pltpu.VMEM((CAP, 2, N, N), jnp.bfloat16),
            pltpu.SemaphoreType.DMA((CAP,)),
            pltpu.SemaphoreType.DMA((CAP * 16,)),
        ],
        compiler_params=pltpu.CompilerParams(vmem_limit_bytes=VMEM_LIMIT),
        name="squares",
    )(owner_map, got0, got1)


def shards(recorded, owner_map):
    bands = jnp.arange(NF, dtype=jnp.int32)[None, :]
    hit = owner_map[None, :] == jnp.arange(NDEV, dtype=jnp.int32)[:, None]
    lowest = jnp.min(jnp.where(hit, bands, NF - 1), axis=1)
    highest = jnp.max(jnp.where(hit, bands, 0), axis=1)
    table = jnp.stack([lowest, highest])
    got0, got1 = tiles_at_owners(recorded, table)
    return squares_of(owner_map, got0, got1)


def solution(mesh):
    in_specs = (P("src", "rcv", None), P())
    out_specs = P(("src", "rcv"), None, None, None, None)
    return jax.shard_map(shards, mesh=mesh, in_specs=in_specs, out_specs=out_specs, check_vma=False)
```

```python
import functools
import math

import jax
import jax.numpy as jnp
import numpy as np
from jax import lax
from jax.experimental import pallas as pl
from jax.experimental.pallas import tpu as pltpu
from jax.sharding import PartitionSpec as P

FIRST = 4
CAP = 2
WATER = 0.5
NT = 512
NF = 64
N = 1024
NDEV = 128
TILES = NDEV + 8
CHUNK = 16
BLOCKS = (4, 4, 2, 256, 256)
STEPS = 64 // CHUNK
VMEM_LIMIT = 62 * 1024 * 1024
MESH = pl.DeviceIdType.MESH


def basis_parts():
    t = np.arange(NT)[:, None]
    f = np.arange(NF)[None, :] + FIRST
    angles = 2.0 * math.pi * ((t * f) % NT) / NT
    both = np.concatenate([np.cos(angles), -np.sin(angles)], axis=1) / math.sqrt(NT)
    high = both.astype(jnp.bfloat16)
    low = (both - high.astype(np.float64)).astype(jnp.bfloat16)
    return np.concatenate([high, low], axis=1)


def merge(own, mirror):
    def power(v):
        square = v * v
        return square + pltpu.roll(square, 64, axis=square.ndim - 1)

    p_own, p_mirror = power(own), power(mirror)
    inv = 1.0 / (p_own + p_mirror + WATER)
    return ((p_own + 0.5 * WATER) * own + (p_mirror + 0.5 * WATER) * mirror) * inv


def count_owned(owner_ref):
    me = lax.axis_index("src") * 16 + lax.axis_index("rcv")
    return lax.fori_loop(0, NF, lambda f, n: n + jnp.where(owner_ref[f] == me, 1, 0), 0)


def block_copy(res, out, sems, row, col):
    r = pl.multiple_of(row * 256, 256)
    c = pl.multiple_of(col * 256, 256)
    return pltpu.make_async_copy(
        res.at[row, col],
        out.at[:, pl.ds(r, 256), pl.ds(c, 256)],
        sems.at[row * 4 + col],
    )


def all_blocks(do):
    @pl.loop(0, 4)
    def _(row):
        @pl.loop(0, 4)
        def _(col):
            do(row, col)


def assemble(got, mat):
    low = lax.broadcasted_iota(jnp.int32, (64, 128), 1) < 64

    def swap(v):
        return pltpu.roll(v, 64, axis=1)

    def put(a, b, top, bottom):
        ra = pl.multiple_of(a * 128, 128)
        rb = pl.multiple_of(b * 128, 128)
        for c in range(2):
            mat[c, pl.ds(ra, 64), pl.ds(rb, 128)] = top[c].astype(jnp.bfloat16)
            mat[c, pl.ds(ra + 64, 64), pl.ds(rb, 128)] = bottom[c].astype(jnp.bfloat16)

    def tile(k):
        return got[k].astype(jnp.float32)

    def pair(a, b):
        t00, t11 = tile(b * 16 + 2 * a), tile(b * 16 + 2 * a + 1)
        u01, u10 = tile(a * 16 + 2 * b + 1), tile(a * 16 + 2 * b)
        turned = jnp.concatenate([u01, u10], axis=0).T
        real, imag = swap(turned[:64]), swap(turned[64:])
        top = (jnp.where(low, t00, real), jnp.where(low, swap(t00), imag))
        bottom = (jnp.where(low, real, swap(t11)), jnp.where(low, imag, t11))
        put(a, b, top, bottom)
        turned = jnp.concatenate([t00, t11], axis=0).T
        real, imag = turned[:64], turned[64:]
        top = (jnp.where(low, real, swap(u10)), jnp.where(low, imag, u10))
        bottom = (jnp.where(low, u01, real), jnp.where(low, swap(u01), imag))
        put(b, a, top, bottom)

    def diagonal(b):
        d0, d1, u = tile(b * 16 + 2 * b), tile(NDEV + b), tile(b * 16 + 2 * b + 1)
        both = jnp.concatenate([d0, d1], axis=0).T
        d0 = merge(d0, jnp.where(low, both[:64], swap(both[64:])))
        d1 = merge(d1, jnp.where(low, swap(both[:64]), both[64:]))
        other = jnp.concatenate([u, u], axis=0).T
        top = (jnp.where(low, d0, other[:64]), jnp.where(low, swap(d0), other[64:]))
        bottom = (jnp.where(low, u, swap(d1)), jnp.where(low, swap(u), d1))
        put(b, b, top, bottom)

    @pl.loop(0, 4)
    def _(b):
        @pl.loop(0, b)
        def _(a):
            for da in range(2):
                for db in range(2):
                    pair(2 * a + da, 2 * b + db)

        pair(2 * b, 2 * b + 1)
        diagonal(2 * b)
        diagonal(2 * b + 1)


def multiply(mat, res, finish):
    @pl.loop(0, 4)
    def _(col):
        cc = pl.multiple_of(col * 256, 256)

        @pl.loop(0, col + 1)
        def _(row):
            rr = pl.multiple_of(row * 256, 256)

            def dot(left, right):
                return jnp.dot(
                    mat[left, pl.ds(rr, 256), :],
                    mat[right, :, pl.ds(cc, 256)],
                    preferred_element_type=jnp.float32,
                )

            factor = 1.0 / math.sqrt(N)
            real = (dot(0, 0) - dot(1, 1)) * factor
            imag = (dot(0, 1) + dot(1, 0)) * factor
            for c, part in enumerate((real, imag)):
                res[row, col, c] = part.astype(jnp.bfloat16)
                res[col, row, c] = part.T.astype(jnp.bfloat16)
            finish(row, col)

            @pl.when(row != col)
            def _():
                finish(col, row)


def peer(k, x, y, z, c):
    dx = k % 4
    dy = (k // 4 + dx) % 4
    dz = (k // 16 + dy) % 4
    xs, ys, zs, cs = (x + dx) % 4, (y + dy) % 4, (z + dz) % 4, (c + k // 64) % 2
    return ys * 2 + cs, xs * 4 + zs


def away_half(i, q):
    return jnp.where(q > 2 * i + 1, q % 2, jnp.where(q < 2 * i, 1 - q % 2, 1))


def exchange_kernel(
    lowest, highest, x_hbm, basis_ref, out, got1,
    xa, xb, wide, turned, kept, sent, mirror, relay, select, extra, got0, mat, res,
    load_a, load_b, send_m, recv_m, send_r, recv_r, send_o, recv_o, send_e, out_sem,
):
    i, q = lax.axis_index("src"), lax.axis_index("rcv")
    y, c = i // 2, i % 2
    x, z = q // 4, q % 4
    me = i * 16 + q
    first = q == 2 * i
    second = q == 2 * i + 1
    far = (x + 2) % 4 == y
    away = away_half(i, q)
    keep = 1 - away
    got = (got0, got1)
    table = (lowest, highest)

    barrier = pltpu.get_barrier_semaphore()

    @pl.loop(1, NDEV)
    def _(k):
        pl.semaphore_signal(barrier, inc=1, device_id=peer(k, x, y, z, c), device_id_type=MESH)

    def fetch_a(k):
        src = x_hbm.at[pl.ds(64 * away + CHUNK * k, CHUNK)]
        return pltpu.make_async_copy(src, xa.at[k % 2], load_a.at[k % 2])

    def fetch_b(k):
        src = x_hbm.at[pl.ds(64 * keep, 64), pl.ds(CHUNK * k, CHUNK)]
        return pltpu.make_async_copy(src, xb.at[k % 2], load_b.at[k % 2])

    for k in range(2):
        fetch_a(k).start()
    for k in range(2):
        fetch_b(k).start()

    ch = 2 * NF

    def transform(values):
        high = values.astype(jnp.bfloat16)
        low = (values - high.astype(jnp.float32)).astype(jnp.bfloat16)
        one = jnp.dot(high, basis_ref[...], preferred_element_type=jnp.float32)
        two = jnp.dot(low, basis_ref[:, :ch], preferred_element_type=jnp.float32)
        wide[...] = one[:, :ch] + one[:, ch:] + two

    def turn(rows_of, out):
        low_half = lax.broadcasted_iota(jnp.int32, (NF, 128), 1) < 64
        for j in range(CHUNK // 2):
            both = rows_of(j).T
            real, imag = both[:NF], both[NF:]
            turned[pl.ds(2 * j, NF, stride=CHUNK), :] = jnp.where(low_half, real, pltpu.roll(imag, 64, axis=1))
            turned[pl.ds(2 * j + 1, NF, stride=CHUNK), :] = jnp.where(low_half, pltpu.roll(real, 64, axis=1), imag)
        out[...] = turned[...].reshape(NF, CHUNK, 128).astype(jnp.bfloat16)

    def mirror_copy(k):
        return pltpu.make_async_remote_copy(
            src_ref=sent.at[k],
            dst_ref=mirror.at[k],
            send_sem=send_m.at[k],
            recv_sem=recv_m.at[k],
            device_id=(q // 2, 2 * i + away),
            device_id_type=MESH,
        )

    def relay_in(k):
        step = 1 + 2 * (k % 2)
        xs, ys = (x + step) % 4, (y + step) % 4
        return pltpu.make_async_remote_copy(
            src_ref=sent.at[k],
            dst_ref=relay.at[k],
            send_sem=send_m.at[k],
            recv_sem=recv_r.at[k],
            device_id=(ys * 2 + c, xs * 4 + z),
            device_id_type=MESH,
        )

    def relay_out(k):
        step = 3 - 2 * (k % 2)
        i_from, q_from = ((y + step) % 4) * 2 + c, ((x + step) % 4) * 4 + z
        return pltpu.make_async_remote_copy(
            src_ref=relay.at[k],
            dst_ref=mirror.at[k],
            send_sem=send_r.at[k],
            recv_sem=recv_m.at[k],
            device_id=(q_from // 2, 2 * i_from + away_half(i_from, q_from)),
            device_id_type=MESH,
        )

    near = jnp.logical_not(jnp.logical_or(second, far))

    @pl.loop(0, STEPS)
    def _(k):
        fetch_a(k).wait()
        transform(xa[k % 2].reshape(CHUNK * 64, NT))

        @pl.when(k + 2 < STEPS)
        def _():
            fetch_a(k + 2).start()

        turn(lambda j: wide[pl.ds(128 * j, 128), :], sent.at[k])

        @pl.when(k == 0)
        def _():
            pl.semaphore_wait(barrier, NDEV - 1)

        @pl.when(near)
        def _():
            mirror_copy(k).start()

        @pl.when(far)
        def _():
            relay_in(k).start()

    def strided(j):
        parts = [wide[pl.ds(2 * j + h, 64, stride=CHUNK), :] for h in range(2)]
        return jnp.concatenate(parts, axis=0)

    @pl.loop(0, STEPS)
    def _(k):
        fetch_b(k).wait()
        transform(xb[k % 2].reshape(CHUNK * 64, NT))

        @pl.when(k + 2 < STEPS)
        def _():
            fetch_b(k + 2).start()

        turn(strided, kept.at[:, pl.ds(pl.multiple_of(k * CHUNK, CHUNK), CHUNK), :])

        @pl.when(far)
        def _():
            relay_in(k).wait_recv()
            relay_out(k).start()

    @pl.when(jnp.logical_not(first))
    def _():
        @pl.loop(0, STEPS)
        def _(k):
            mirror_copy(k).wait_recv()
            rows = pl.ds(pl.multiple_of(k * CHUNK, CHUNK), CHUNK)

            @pl.loop(0, NF // 4)
            def _(f):
                own = kept[pl.ds(f * 4, 4), rows, :].astype(jnp.float32)
                other = mirror[k, pl.ds(f * 4, 4)].astype(jnp.float32)
                kept[pl.ds(f * 4, 4), rows, :] = merge(own, other).astype(jnp.bfloat16)

    def extra_copy(slot, k):
        device = peer(k, x, y, z, c)
        return pltpu.make_async_remote_copy(
            src_ref=extra.at[slot, device[0] * 16 + device[1]],
            dst_ref=got[slot].at[NDEV + i],
            send_sem=send_e.at[slot],
            recv_sem=recv_o.at[slot],
            device_id=device,
            device_id_type=MESH,
        )

    def owner_copy(slot, k):
        device = peer(k, x, y, z, c)
        return pltpu.make_async_remote_copy(
            src_ref=select.at[slot, device[0] * 16 + device[1]],
            dst_ref=got[slot].at[me],
            send_sem=send_o.at[slot],
            recv_sem=recv_o.at[slot],
            device_id=device,
            device_id_type=MESH,
        )

    def local_copies(slot):
        own = pltpu.make_async_copy(select.at[slot, me], got[slot].at[me], recv_o.at[slot])
        more = pltpu.make_async_copy(extra.at[slot, me], got[slot].at[NDEV + i], recv_o.at[slot])
        return own, more

    for slot in range(CAP):
        @pl.loop(0, NDEV)
        def _(d):
            select[slot, d] = kept[table[slot][d]]

        @pl.when(second)
        def _():
            @pl.loop(0, NDEV)
            def _(d):
                f = table[slot][d]
                for k in range(STEPS):
                    extra[slot, d, k * CHUNK:(k + 1) * CHUNK] = sent[k, f]

    for slot in range(CAP):
        own, more = local_copies(slot)
        own.start()

        @pl.when(jnp.logical_not(second))
        def _():
            @pl.loop(1, NDEV)
            def _(k):
                owner_copy(slot, k).start()

        @pl.when(second)
        def _():
            more.start()

            @pl.loop(1, NDEV)
            def _(k):
                owner_copy(slot, k).start()
                extra_copy(slot, k).start()

    @pl.when(near)
    def _():
        @pl.loop(0, STEPS)
        def _(k):
            mirror_copy(k).wait_send()

    @pl.when(far)
    def _():
        @pl.loop(0, STEPS)
        def _(k):
            relay_in(k).wait_send()
            relay_out(k).wait_send()

    def receive(slot):
        pltpu.make_async_copy(got[slot], got[slot], recv_o.at[slot]).wait()

    receive(0)
    assemble(got0, mat)
    multiply(mat, res, lambda row, col: None)
    whole = pltpu.make_async_copy(res, out, out_sem)
    whole.start()

    for slot in range(CAP):
        most = select.at[slot, pl.ds(0, NDEV - 1)]
        pltpu.make_async_copy(most, most, send_o.at[slot]).wait()

        @pl.when(second)
        def _():
            pltpu.make_async_copy(most, most, send_e.at[slot]).wait()

    receive(1)
    whole.wait()


def tiles_at_owners(recorded, lowest, highest):
    tile = (64, 128)
    dma = pltpu.SemaphoreType.DMA
    return pl.pallas_call(
        exchange_kernel,
        out_shape=[
            jax.ShapeDtypeStruct(BLOCKS, jnp.bfloat16),
            jax.ShapeDtypeStruct((TILES,) + tile, jnp.bfloat16),
        ],
        in_specs=[pl.BlockSpec(memory_space=pltpu.SMEM)] * 2 + [
            pl.BlockSpec(memory_space=pl.ANY),
            pl.BlockSpec(memory_space=pltpu.VMEM),
        ],
        out_specs=[pl.BlockSpec(memory_space=pl.ANY)] * 2,
        scratch_shapes=[
            pltpu.VMEM((2, CHUNK, 64, NT), jnp.float32),
            pltpu.VMEM((2, 64, CHUNK, NT), jnp.float32),
            pltpu.VMEM((CHUNK * 64, 2 * NF), jnp.float32),
            pltpu.VMEM((NF * CHUNK, 128), jnp.float32),
            pltpu.VMEM((NF,) + tile, jnp.bfloat16),
            pltpu.VMEM((STEPS, NF, CHUNK, 128), jnp.bfloat16),
            pltpu.VMEM((STEPS, NF, CHUNK, 128), jnp.bfloat16),
            pltpu.VMEM((STEPS, NF, CHUNK, 128), jnp.bfloat16),
            pltpu.VMEM((CAP, NDEV) + tile, jnp.bfloat16),
            pltpu.VMEM((CAP, NDEV) + tile, jnp.bfloat16),
            pltpu.VMEM((TILES,) + tile, jnp.bfloat16),
            pltpu.VMEM((2, N, N), jnp.bfloat16),
            pltpu.VMEM(BLOCKS, jnp.bfloat16),
            dma((2,)), dma((2,)), dma((STEPS,)), dma((STEPS,)), dma((STEPS,)), dma((STEPS,)),
            dma((CAP,)), dma((CAP,)), dma((CAP,)), dma,
        ],
        compiler_params=pltpu.CompilerParams(
            vmem_limit_bytes=VMEM_LIMIT, collective_id=0, has_side_effects=True
        ),
        name="exchange",
    )(lowest, highest, recorded, jnp.asarray(basis_parts()))


def square_kernel(owner_ref, got1, half, out, got, mat, res, first, sem_in, sem_half, sems_half, sems):
    mine = count_owned(owner_ref)
    half_in = pltpu.make_async_copy(half, first, sem_half)
    half_in.start()

    def copy_out(row, col):
        return block_copy(res, out.at[0, 1], sems, row, col)

    def half_out(row, col):
        return block_copy(first, out.at[0, 0], sems_half, row, col)

    def finish_half():
        half_in.wait()

        @pl.when(mine == 0)
        def _():
            first[...] = jnp.zeros(BLOCKS, jnp.bfloat16)

        all_blocks(lambda row, col: half_out(row, col).start())

    def empty():
        res[...] = jnp.zeros(BLOCKS, jnp.bfloat16)
        finish_half()
        all_blocks(lambda row, col: copy_out(row, col).start())

    def owned():
        load = pltpu.make_async_copy(got1, got, sem_in)
        load.start()
        load.wait()
        assemble(got, mat)
        finish_half()
        multiply(mat, res, lambda row, col: copy_out(row, col).start())

    lax.cond(mine == 2, owned, empty)
    all_blocks(lambda row, col: copy_out(row, col).wait())
    all_blocks(lambda row, col: half_out(row, col).wait())


def squares_of(owner_map, got1, half_done):
    return pl.pallas_call(
        square_kernel,
        out_shape=jax.ShapeDtypeStruct((1, CAP, 2, N, N), jnp.bfloat16),
        in_specs=[pl.BlockSpec(memory_space=pltpu.SMEM)] + [pl.BlockSpec(memory_space=pl.ANY)] * 2,
        out_specs=pl.BlockSpec(memory_space=pl.ANY),
        scratch_shapes=[
            pltpu.VMEM((TILES, 64, 128), jnp.bfloat16),
            pltpu.VMEM((2, N, N), jnp.bfloat16),
            pltpu.VMEM(BLOCKS, jnp.bfloat16),
            pltpu.VMEM(BLOCKS, jnp.bfloat16),
            pltpu.SemaphoreType.DMA,
            pltpu.SemaphoreType.DMA,
            pltpu.SemaphoreType.DMA((16,)),
            pltpu.SemaphoreType.DMA((16,)),
        ],
        compiler_params=pltpu.CompilerParams(vmem_limit_bytes=VMEM_LIMIT),
        name="squares",
    )(owner_map, got1, half_done)


def shards(recorded, owner_map):
    bands = jnp.arange(NF, dtype=jnp.int32)[None, :]
    hit = owner_map[None, :] == jnp.arange(NDEV, dtype=jnp.int32)[:, None]
    lowest = jnp.min(jnp.where(hit, bands, NF - 1), axis=1)
    highest = jnp.max(jnp.where(hit, bands, 0), axis=1)
    half_done, got1 = tiles_at_owners(recorded, lowest, highest)
    return squares_of(owner_map, got1, half_done)


def solution(mesh):
    in_specs = (P("src", "rcv", None), P())
    out_specs = P(("src", "rcv"), None, None, None, None)
    return jax.shard_map(shards, mesh=mesh, in_specs=in_specs, out_specs=out_specs, check_vma=False)
```

```python
import functools
import math

import jax
import jax.numpy as jnp
import numpy as np
from jax import lax
from jax.experimental import pallas as pl
from jax.experimental.pallas import tpu as pltpu
from jax.sharding import PartitionSpec as P

FIRST = 4
CAP = 2
WATER = 0.5
NT = 512
NF = 64
N = 1024
NDEV = 128
TILES = NDEV + 8
CHUNK = 16
BLOCKS = (4, 4, 2, 256, 256)
STEPS = 64 // CHUNK
VMEM_LIMIT = 62 * 1024 * 1024
MESH = pl.DeviceIdType.MESH


def basis_parts():
    t = np.arange(NT)[:, None]
    f = np.arange(NF)[None, :] + FIRST
    angles = 2.0 * math.pi * ((t * f) % NT) / NT
    both = np.concatenate([np.cos(angles), -np.sin(angles)], axis=1) / math.sqrt(NT)
    high = both.astype(jnp.bfloat16)
    low = (both - high.astype(np.float64)).astype(jnp.bfloat16)
    return np.concatenate([high, low], axis=1)


def merge(own, mirror):
    def power(v):
        square = v * v
        return square + pltpu.roll(square, 64, axis=square.ndim - 1)

    p_own, p_mirror = power(own), power(mirror)
    inv = 1.0 / (p_own + p_mirror + WATER)
    return ((p_own + 0.5 * WATER) * own + (p_mirror + 0.5 * WATER) * mirror) * inv


def count_owned(owner_ref):
    me = lax.axis_index("src") * 16 + lax.axis_index("rcv")
    return lax.fori_loop(0, NF, lambda f, n: n + jnp.where(owner_ref[f] == me, 1, 0), 0)


def block_copy(res, out, sems, row, col):
    r = pl.multiple_of(row * 256, 256)
    c = pl.multiple_of(col * 256, 256)
    return pltpu.make_async_copy(
        res.at[row, col],
        out.at[:, pl.ds(r, 256), pl.ds(c, 256)],
        sems.at[row * 4 + col],
    )


def all_blocks(do):
    @pl.loop(0, 4)
    def _(row):
        @pl.loop(0, 4)
        def _(col):
            do(row, col)


def assemble(got, mat):
    low = lax.broadcasted_iota(jnp.int32, (64, 128), 1) < 64

    def swap(v):
        return pltpu.roll(v, 64, axis=1)

    def put(a, b, top, bottom):
        ra = pl.multiple_of(a * 128, 128)
        rb = pl.multiple_of(b * 128, 128)
        for c in range(2):
            mat[c, pl.ds(ra, 64), pl.ds(rb, 128)] = top[c]
            mat[c, pl.ds(ra + 64, 64), pl.ds(rb, 128)] = bottom[c]

    def tile(k):
        return got[k]

    def merged(own, mirror):
        return merge(own.astype(jnp.float32), mirror.astype(jnp.float32)).astype(jnp.bfloat16)

    def pair(a, b):
        t00, t11 = tile(b * 16 + 2 * a), tile(b * 16 + 2 * a + 1)
        u01, u10 = tile(a * 16 + 2 * b + 1), tile(a * 16 + 2 * b)
        turned = jnp.concatenate([u01, u10], axis=0).T
        real, imag = swap(turned[:64]), swap(turned[64:])
        top = (jnp.where(low, t00, real), jnp.where(low, swap(t00), imag))
        bottom = (jnp.where(low, real, swap(t11)), jnp.where(low, imag, t11))
        put(a, b, top, bottom)
        turned = jnp.concatenate([t00, t11], axis=0).T
        real, imag = turned[:64], turned[64:]
        top = (jnp.where(low, real, swap(u10)), jnp.where(low, imag, u10))
        bottom = (jnp.where(low, u01, real), jnp.where(low, swap(u01), imag))
        put(b, a, top, bottom)

    def diagonal(b):
        d0, d1, u = tile(b * 16 + 2 * b), tile(NDEV + b), tile(b * 16 + 2 * b + 1)
        both = jnp.concatenate([d0, d1], axis=0).T
        d0 = merged(d0, jnp.where(low, both[:64], swap(both[64:])))
        d1 = merged(d1, jnp.where(low, swap(both[:64]), both[64:]))
        other = jnp.concatenate([u, u], axis=0).T
        top = (jnp.where(low, d0, other[:64]), jnp.where(low, swap(d0), other[64:]))
        bottom = (jnp.where(low, u, swap(d1)), jnp.where(low, swap(u), d1))
        put(b, b, top, bottom)

    @pl.loop(0, 4)
    def _(b):
        @pl.loop(0, b)
        def _(a):
            for da in range(2):
                for db in range(2):
                    pair(2 * a + da, 2 * b + db)

        pair(2 * b, 2 * b + 1)
        diagonal(2 * b)
        diagonal(2 * b + 1)


def multiply(mat, res, finish):
    @pl.loop(0, 4)
    def _(col):
        cc = pl.multiple_of(col * 256, 256)

        @pl.loop(0, col + 1)
        def _(row):
            rr = pl.multiple_of(row * 256, 256)

            left = mat[:, pl.ds(rr, 256), :].reshape(512, N)
            with_real, with_imag = [
                jnp.dot(left, mat[c, :, pl.ds(cc, 256)], preferred_element_type=jnp.float32)
                for c in range(2)
            ]
            factor = 1.0 / math.sqrt(N)
            real = (with_real[:256] - with_imag[256:]) * factor
            imag = (with_imag[:256] + with_real[256:]) * factor
            for c, part in enumerate((real, imag)):
                part = part.astype(jnp.bfloat16)
                res[row, col, c] = part
                res[col, row, c] = part.T
            finish(row, col)

            @pl.when(row != col)
            def _():
                finish(col, row)


def peer(k, x, y, z, c):
    k = lax.rem(33 * k, 128)
    dx = lax.rem(k, 4)
    dy = lax.rem(lax.div(k, 4) + 2 * dx, 4)
    dz = lax.rem(lax.div(k, 16) + 2 * dy, 4)
    xs, ys, zs = lax.rem(x + dx, 4), lax.rem(y + dy, 4), lax.rem(z + dz, 4)
    return ys * 2 + lax.rem(c + lax.div(k, 64), 2), xs * 4 + zs


def away_half(i, q):
    return jnp.where(q > 2 * i + 1, q % 2, jnp.where(q < 2 * i, 1 - q % 2, 1))


def exchange_kernel(
    lowest, highest, x_hbm, basis_ref, out, got1,
    xa, xb, wide, turned, kept, sent, mirror, relay, select, extra, share, got0, mat, res,
    load_a, load_b, send_m, recv_m, send_r, recv_r, recv_s, send_o, recv_o, send_e, out_sem,
):
    i, q = lax.axis_index("src"), lax.axis_index("rcv")
    y, c = i // 2, i % 2
    x, z = q // 4, q % 4
    me = i * 16 + q
    first = q == 2 * i
    second = q == 2 * i + 1
    far = (x + 2) % 4 == y
    apart = lax.rem(q + 31 - 2 * i, 16)
    helper = lax.rem(apart, 4) == 0
    share_rows = pl.ds(pl.multiple_of(lax.div(apart, 4) * CHUNK, CHUNK), CHUNK)
    away = away_half(i, q)
    keep = 1 - away
    got = (got0, got1)
    table = (lowest, highest)

    barrier = pltpu.get_barrier_semaphore()

    def fetch_a(k):
        src = x_hbm.at[pl.ds(64 * away + CHUNK * k, CHUNK)]
        return pltpu.make_async_copy(src, xa.at[k % 2], load_a.at[k % 2])

    def fetch_b(k):
        src = x_hbm.at[pl.ds(64 * keep, 64), pl.ds(CHUNK * k, CHUNK)]
        return pltpu.make_async_copy(src, xb.at[k % 2], load_b.at[k % 2])

    for k in range(2):
        fetch_a(k).start()
    for k in range(2):
        fetch_b(k).start()

    others = [lax.rem(i + step, 8) for step in range(8)]

    def greet(first_step, column):
        for src in others[first_step:]:
            pl.semaphore_signal(barrier, inc=1, device_id=(src, column), device_id_type=MESH)

    greet(1, q)

    @pl.loop(1, 16)
    def _(step):
        greet(0, lax.rem(q + step, 16))

    ch = 2 * NF

    def transform(values):
        high = values.astype(jnp.bfloat16)
        low = (values - high.astype(jnp.float32)).astype(jnp.bfloat16)
        one = jnp.dot(high, basis_ref[...], preferred_element_type=jnp.float32)
        two = jnp.dot(low, basis_ref[:, :ch], preferred_element_type=jnp.float32)
        wide[...] = one[:, :ch] + one[:, ch:] + two

    def turn(rows_of, out):
        low_half = lax.broadcasted_iota(jnp.int32, (NF, 128), 1) < 64
        for j in range(CHUNK // 2):
            both = rows_of(j).T
            real, imag = both[:NF], both[NF:]
            turned[pl.ds(2 * j, NF, stride=CHUNK), :] = jnp.where(low_half, real, pltpu.roll(imag, 64, axis=1))
            turned[pl.ds(2 * j + 1, NF, stride=CHUNK), :] = jnp.where(low_half, pltpu.roll(real, 64, axis=1), imag)
        out[...] = turned[...].reshape(NF, CHUNK, 128).astype(jnp.bfloat16)

    def mirror_copy(k):
        return pltpu.make_async_remote_copy(
            src_ref=sent.at[k],
            dst_ref=mirror.at[k],
            send_sem=send_m.at[k],
            recv_sem=recv_m.at[k],
            device_id=(q // 2, 2 * i + away),
            device_id_type=MESH,
        )

    def relay_in(k):
        step = 1 + 2 * (k % 2)
        xs, ys = (x + step) % 4, (y + step) % 4
        return pltpu.make_async_remote_copy(
            src_ref=sent.at[k],
            dst_ref=relay.at[k],
            send_sem=send_m.at[k],
            recv_sem=recv_r.at[k],
            device_id=(ys * 2 + c, xs * 4 + z),
            device_id_type=MESH,
        )

    def relay_out(k):
        step = 3 - 2 * (k % 2)
        i_from, q_from = ((y + step) % 4) * 2 + c, ((x + step) % 4) * 4 + z
        return pltpu.make_async_remote_copy(
            src_ref=relay.at[k],
            dst_ref=mirror.at[k],
            send_sem=send_r.at[k],
            recv_sem=recv_m.at[k],
            device_id=(q_from // 2, 2 * i_from + away_half(i_from, q_from)),
            device_id_type=MESH,
        )

    near = jnp.logical_not(jnp.logical_or(second, far))

    def share_copy(k):
        return pltpu.make_async_remote_copy(
            src_ref=sent.at[k],
            dst_ref=share,
            send_sem=send_m.at[k],
            recv_sem=recv_s,
            device_id=(i, lax.rem(q + 4 * k, 16)),
            device_id_type=MESH,
        )

    kept_share = pltpu.make_async_copy(sent.at[0], share, recv_s)

    @pl.loop(0, STEPS)
    def _(k):
        fetch_a(k).wait()
        transform(xa[k % 2].reshape(CHUNK * 64, NT))

        @pl.when(k + 2 < STEPS)
        def _():
            fetch_a(k + 2).start()

        turn(lambda j: wide[pl.ds(128 * j, 128), :], sent.at[k])

        @pl.when(k == 0)
        def _():
            pl.semaphore_wait(barrier, NDEV - 1)

        @pl.when(near)
        def _():
            mirror_copy(k).start()

        @pl.when(far)
        def _():
            relay_in(k).start()

        @pl.when(jnp.logical_and(second, k == 0))
        def _():
            kept_share.start()

        @pl.when(jnp.logical_and(second, k > 0))
        def _():
            share_copy(k).start()

    def strided(j):
        parts = [wide[pl.ds(2 * j + h, 64, stride=CHUNK), :] for h in range(2)]
        return jnp.concatenate(parts, axis=0)

    @pl.loop(0, STEPS)
    def _(k):
        fetch_b(k).wait()
        transform(xb[k % 2].reshape(CHUNK * 64, NT))

        @pl.when(k + 2 < STEPS)
        def _():
            fetch_b(k + 2).start()

        turn(strided, kept.at[:, pl.ds(pl.multiple_of(k * CHUNK, CHUNK), CHUNK), :])

        @pl.when(far)
        def _():
            relay_in(k).wait_recv()
            relay_out(k).start()

    def merge_chunks(low, high):
        @pl.when(jnp.logical_not(first))
        def _():
            @pl.loop(low, high)
            def _(k):
                mirror_copy(k).wait_recv()
                rows = pl.ds(pl.multiple_of(k * CHUNK, CHUNK), CHUNK)

                @pl.loop(0, NF // 8)
                def _(f):
                    own = kept[pl.ds(f * 8, 8), rows, :].astype(jnp.float32)
                    other = mirror[k, pl.ds(f * 8, 8)].astype(jnp.float32)
                    kept[pl.ds(f * 8, 8), rows, :] = merge(own, other).astype(jnp.bfloat16)

    def extra_copy(slot, k):
        device = peer(k, x, y, z, c)
        return pltpu.make_async_remote_copy(
            src_ref=extra.at[slot, device[0] * 16 + device[1]],
            dst_ref=got[slot].at[NDEV + i, share_rows],
            send_sem=send_e.at[slot],
            recv_sem=recv_o.at[slot],
            device_id=device,
            device_id_type=MESH,
        )

    def owner_copy(slot, k, rows):
        device = peer(k, x, y, z, c)
        return pltpu.make_async_remote_copy(
            src_ref=select.at[slot, device[0] * 16 + device[1], rows],
            dst_ref=got[slot].at[me, rows],
            send_sem=send_o.at[slot],
            recv_sem=recv_o.at[slot],
            device_id=device,
            device_id_type=MESH,
        )

    def send_rows(slot, low, high):
        rows = slice(low, high)

        @pl.loop(0, NDEV // 8)
        def _(group):
            for d in range(8):
                select[slot, group * 8 + d, rows] = kept[table[slot][group * 8 + d], rows]

        @pl.loop(1, NDEV)
        def _(k):
            owner_copy(slot, k, rows).start()

    @pl.when(helper)
    def _():
        pltpu.make_async_copy(share, share, recv_s).wait()
        for slot in range(CAP):
            @pl.loop(0, NDEV // 8)
            def _(group):
                for d in range(8):
                    extra[slot, group * 8 + d] = share[table[slot][group * 8 + d]]

            own = got[slot].at[NDEV + i, share_rows]
            pltpu.make_async_copy(extra.at[slot, me], own, recv_o.at[slot]).start()

            @pl.loop(1, NDEV)
            def _(k):
                extra_copy(slot, k).start()

    merge_chunks(0, 4)
    send_rows(0, 0, 64)
    send_rows(1, 0, 64)
    for slot in range(CAP):
        pltpu.make_async_copy(select.at[slot, me], got[slot].at[me], recv_o.at[slot]).start()

    @pl.when(near)
    def _():
        @pl.loop(0, STEPS)
        def _(k):
            mirror_copy(k).wait_send()

    @pl.when(second)
    def _():
        @pl.loop(1, STEPS)
        def _(k):
            share_copy(k).wait_send()

    @pl.when(far)
    def _():
        @pl.loop(0, STEPS)
        def _(k):
            relay_in(k).wait_send()
            relay_out(k).wait_send()

    def receive(slot):
        pltpu.make_async_copy(got[slot], got[slot], recv_o.at[slot]).wait()

    receive(0)
    assemble(got0, mat)
    multiply(mat, res, lambda row, col: None)
    whole = pltpu.make_async_copy(res, out, out_sem)
    whole.start()

    for slot in range(CAP):
        most = select.at[slot, pl.ds(0, NDEV - 1)]
        pltpu.make_async_copy(most, most, send_o.at[slot]).wait()

        @pl.when(helper)
        def _():
            pieces = extra.at[slot, pl.ds(0, NDEV - 1)]
            pltpu.make_async_copy(pieces, pieces, send_e.at[slot]).wait()

    receive(1)
    whole.wait()


def tiles_at_owners(recorded, lowest, highest):
    tile = (64, 128)
    dma = pltpu.SemaphoreType.DMA
    return pl.pallas_call(
        exchange_kernel,
        out_shape=[
            jax.ShapeDtypeStruct(BLOCKS, jnp.bfloat16),
            jax.ShapeDtypeStruct((TILES,) + tile, jnp.bfloat16),
        ],
        in_specs=[pl.BlockSpec(memory_space=pltpu.SMEM)] * 2 + [
            pl.BlockSpec(memory_space=pl.ANY),
            pl.BlockSpec(memory_space=pltpu.VMEM),
        ],
        out_specs=[pl.BlockSpec(memory_space=pl.ANY)] * 2,
        scratch_shapes=[
            pltpu.VMEM((2, CHUNK, 64, NT), jnp.float32),
            pltpu.VMEM((2, 64, CHUNK, NT), jnp.float32),
            pltpu.VMEM((CHUNK * 64, 2 * NF), jnp.float32),
            pltpu.VMEM((NF * CHUNK, 128), jnp.float32),
            pltpu.VMEM((NF,) + tile, jnp.bfloat16),
            pltpu.VMEM((STEPS, NF, CHUNK, 128), jnp.bfloat16),
            pltpu.VMEM((STEPS, NF, CHUNK, 128), jnp.bfloat16),
            pltpu.VMEM((STEPS, NF, CHUNK, 128), jnp.bfloat16),
            pltpu.VMEM((CAP, NDEV) + tile, jnp.bfloat16),
            pltpu.VMEM((CAP, NDEV, CHUNK, 128), jnp.bfloat16),
            pltpu.VMEM((NF, CHUNK, 128), jnp.bfloat16),
            pltpu.VMEM((TILES,) + tile, jnp.bfloat16),
            pltpu.VMEM((2, N, N), jnp.bfloat16),
            pltpu.VMEM(BLOCKS, jnp.bfloat16),
            dma((2,)), dma((2,)), dma((STEPS,)), dma((STEPS,)), dma((STEPS,)), dma((STEPS,)), dma,
            dma((CAP,)), dma((CAP,)), dma((CAP,)), dma,
        ],
        compiler_params=pltpu.CompilerParams(
            vmem_limit_bytes=VMEM_LIMIT, collective_id=0, has_side_effects=True
        ),
        name="exchange",
    )(lowest, highest, recorded, jnp.asarray(basis_parts()))


def square_kernel(owner_ref, got1, half, out, got, mat, res, first, sem_in, sem_half, sems_half, sems):
    mine = count_owned(owner_ref)
    load = pltpu.make_async_copy(got1, got, sem_in)
    load.start()
    half_in = pltpu.make_async_copy(half, first, sem_half)
    half_in.start()

    def copy_out(row, col):
        return block_copy(res, out.at[0, 1], sems, row, col)

    def half_out(row, col):
        return block_copy(first, out.at[0, 0], sems_half, row, col)

    def finish_half():
        half_in.wait()

        @pl.when(mine == 0)
        def _():
            first[...] = jnp.zeros(BLOCKS, jnp.bfloat16)

        all_blocks(lambda row, col: half_out(row, col).start())

    def empty():
        load.wait()
        res[...] = jnp.zeros(BLOCKS, jnp.bfloat16)
        finish_half()
        all_blocks(lambda row, col: copy_out(row, col).start())

    def owned():
        load.wait()
        assemble(got, mat)
        finish_half()
        multiply(mat, res, lambda row, col: copy_out(row, col).start())

    lax.cond(mine == 2, owned, empty)
    all_blocks(lambda row, col: copy_out(row, col).wait())
    all_blocks(lambda row, col: half_out(row, col).wait())


def squares_of(owner_map, got1, half_done):
    return pl.pallas_call(
        square_kernel,
        out_shape=jax.ShapeDtypeStruct((1, CAP, 2, N, N), jnp.bfloat16),
        in_specs=[pl.BlockSpec(memory_space=pltpu.SMEM)] + [pl.BlockSpec(memory_space=pl.ANY)] * 2,
        out_specs=pl.BlockSpec(memory_space=pl.ANY),
        scratch_shapes=[
            pltpu.VMEM((TILES, 64, 128), jnp.bfloat16),
            pltpu.VMEM((2, N, N), jnp.bfloat16),
            pltpu.VMEM(BLOCKS, jnp.bfloat16),
            pltpu.VMEM(BLOCKS, jnp.bfloat16),
            pltpu.SemaphoreType.DMA,
            pltpu.SemaphoreType.DMA,
            pltpu.SemaphoreType.DMA((16,)),
            pltpu.SemaphoreType.DMA((16,)),
        ],
        compiler_params=pltpu.CompilerParams(vmem_limit_bytes=VMEM_LIMIT),
        name="squares",
    )(owner_map, got1, half_done)


def shards(recorded, owner_map):
    bands = jnp.arange(NF, dtype=jnp.int32)[None, :]
    hit = owner_map[None, :] == jnp.arange(NDEV, dtype=jnp.int32)[:, None]
    lowest = jnp.min(jnp.where(hit, bands, NF - 1), axis=1)
    highest = jnp.max(jnp.where(hit, bands, 0), axis=1)
    half_done, got1 = tiles_at_owners(recorded, lowest, highest)
    return squares_of(owner_map, got1, half_done)


def solution(mesh):
    in_specs = (P("src", "rcv", None), P())
    out_specs = P(("src", "rcv"), None, None, None, None)
    return jax.shard_map(shards, mesh=mesh, in_specs=in_specs, out_specs=out_specs, check_vma=False)
```
